256 devices in a mesh: seq: 64 (over x, z, core), tp: 4 (over y).
Axes of the slice: x: 4, y: 4, z: 8, core: 2. Of those that a mesh axis runs over, the one named last changes fastest.
Arguments:
- queries: bfloat16 [16384, 4096], P('seq', 'tp'), may hold values from -6 to 6
- keys: bfloat16 [16384, 4096], P('seq', 'tp'), may hold values from -6 to 6
- values: bfloat16 [16384, 4096], P('seq', 'tp'), may hold values from -12 to 12
- seeds: bfloat16 [32, 256], P('tp'), may hold values from -6 to 6
- gain: float32 [4096], P('tp'), may hold values from 0.1 to 1.9
Outputs:
- attended: bfloat16 [16384, 4096], P('seq', 'tp')
The draws below stay inside these ranges and needn't reach their ends.
All inputs are finite; a program needn't handle non-finite values.
Results may differ from the reference program's by a relative error of at most 0.009.
Values sent between devices are 32-bit elements; how exact they have to be, the bound alone decides.
A program may use at most 192 MiB of HBM per device.

```python
import jax
import jax.numpy as jnp
from jax import lax

H = 32
E = 128
M = 256
TOKENS = 16384


def draw_values(key, part):
    head = (jnp.arange(H * E) // E).astype(jnp.float32)
    scale = 1.0 + 2.0 * head / (H - 1)
    base = jax.random.truncated_normal(key, -4.0, 4.0, (TOKENS, H * E), jnp.float32)
    return (base * scale[None, :]).astype(jnp.bfloat16)


def block_levels(key, dims, split, smallest, largest):
    factor_of, own = 1.0, jax.random.fold_in(key, 6)
    for dim, parts in split:
        heights = jnp.exp(jax.random.uniform(jax.random.fold_in(own, dim), (parts,), jnp.float32, smallest / len(split), largest / len(split)))
        factor_of = factor_of * jnp.repeat(heights, dims[dim] // parts).reshape([-1 if axis == dim else 1 for axis in range(len(dims))])
    return factor_of


def scatter_about(stream_key, dims, scale, most, pieces=(), kind=jnp.bfloat16):
    entries = scale * jax.random.normal(stream_key, dims, jnp.float32)
    if pieces:
        entries = entries * block_levels(stream_key, dims, pieces, -0.22, 0.18)
    return jnp.clip(entries, -most, most).astype(kind)


def setup_inputs(seed: int = 0) -> dict:
    splits = jax.random.split(jax.random.key(seed), 6)
    queries = scatter_about(splits[0], (TOKENS, H * E), 1.0, 6.0, ((0, 64), (1, 4)))
    keys = scatter_about(splits[1], (TOKENS, H * E), 1.0, 6.0, ((0, 64), (1, 4)))
    values = draw_values(jax.random.fold_in(splits[5], 71), 0)
    seeds = scatter_about(splits[3], (H, M), 1.0, 6.0, ((0, 4),))
    gain = jnp.clip(1.0 + 0.18 * jax.random.normal(splits[4], (H * E,), jnp.float32), 0.1, 1.9)
    return {"queries": queries, "keys": keys, "values": values, "seeds": seeds, "gain": gain}


def features(rows, seeds):
    count = rows.shape[0]
    x = rows.astype(jnp.float32).reshape(count, H, E)
    blocks = seeds.astype(jnp.float32).reshape(H, M // E, E)
    spectrum = jnp.fft.fft(blocks)[None] * jnp.fft.fft(x)[:, :, None, :]
    mixed = jnp.real(jnp.fft.ifft(spectrum)).reshape(count, H, M) * E ** (-0.25)
    return (jax.nn.elu(mixed) + 1.0).astype(jnp.bfloat16)

def reference(queries, keys, values, seeds, gain):
    block = min(512, TOKENS)
    steps_count = TOKENS // block
    q_blocks = queries.reshape(steps_count, block, H * E)
    k_blocks = keys.reshape(steps_count, block, H * E)
    v_blocks = values.reshape(steps_count, block, H * E)
    causal = jnp.tril(jnp.ones((block, block), dtype=bool))
    high = lax.Precision.HIGHEST

    def advance(carry, inputs):
        state, totals = carry
        q_rows, k_rows, v_rows = inputs
        fq = features(q_rows, seeds).astype(jnp.float32)
        fk = features(k_rows, seeds).astype(jnp.float32)
        vals = v_rows.astype(jnp.float32).reshape(block, H, E)
        scores = jnp.einsum('bhm,chm->hbc', fq, fk, precision=high)
        scores = jnp.where(causal[None], scores, 0.0)
        wscores = lax.optimization_barrier(scores.astype(jnp.bfloat16)).astype(jnp.float32)
        num = jnp.einsum('hbc,che->bhe', wscores, vals, precision=high)
        num = num + jnp.einsum('bhm,hme->bhe', fq, state, precision=high)
        den = lax.optimization_barrier(jnp.sum(scores, axis=2)).T + jnp.einsum('bhm,hm->bh', fq, totals, precision=high)
        heads = num / den[:, :, None]
        meansq = lax.optimization_barrier(jnp.mean(heads * heads, axis=(1, 2)))
        normed = heads.reshape(block, H * E) * lax.rsqrt(meansq + 1e-06)[:, None] * gain[None, :]
        state = state + jnp.einsum('chm,che->hme', fk, vals, precision=high)
        totals = totals + lax.optimization_barrier(jnp.sum(fk, axis=0))
        return ((state, totals), normed.astype(jnp.bfloat16))
    start = (jnp.zeros((H, M, E), jnp.float32), jnp.zeros((H, M), jnp.float32))
    _, outputs = lax.scan(advance, start, (q_blocks, k_blocks, v_blocks))
    return outputs.reshape(TOKENS, H * E)
```

```python
import functools

import jax
import jax.numpy as jnp
from jax import lax
from jax.experimental import pallas as pl
from jax.experimental.pallas import tpu as pltpu
from jax.sharding import PartitionSpec as P

XS, ZS, CORES, YS = 4, 8, 2, 4
F32, BF16 = jnp.float32, jnp.bfloat16


def remote(src, dst, send, recv, **where):
    return pltpu.make_async_remote_copy(
        src_ref=src,
        dst_ref=dst,
        send_sem=send,
        recv_sem=recv,
        device_id=where,
        device_id_type=pl.DeviceIdType.MESH,
    )


def features(x, table, scale):
    u = jnp.dot(x, table, preferred_element_type=F32) * scale
    return (jnp.maximum(u, 0.0) + jnp.exp(jnp.minimum(u, 0.0))).astype(BF16)


def kernel(
    q_hbm,
    k_hbm,
    v_hbm,
    seeds_ref,
    gain_ref,
    out_ref,
    q,
    k,
    v,
    seedf,
    table,
    fk,
    fq,
    numden,
    heads,
    own,
    got,
    chip,
    up,
    across,
    down,
    back,
    pass_on,
    full,
    tot,
    tot_got,
    tot_chip,
    tot_up,
    tot_row,
    tot_across,
    tot_half,
    norm,
    norm_got,
    load_sem,
    pair_s,
    pair_r,
    up_s,
    up_r,
    x_s,
    x_r,
    down_s,
    down_r,
    fwd_s,
    fwd_r,
    tp_s,
    tp_r,
    tu_s,
    tu_r,
    tx_s,
    tx_r,
    th_s,
    th_r,
    n_s,
    n_r,
):
    tok, columns = q.shape
    heads_here, _, feats = fk.shape
    width = columns // heads_here
    per = heads_here // 2
    rows = own.shape[3]
    scale = width ** (-0.25)
    s = lax.axis_index("seq")
    y = lax.axis_index("tp")
    c = s % CORES
    z = (s // CORES) % ZS
    x = s // (CORES * ZS)
    o = 1 - c

    def at(x_, z_, c_):
        return (x_ * ZS + z_) * CORES + c_

    partner = at(x, z, o)

    def zpeer(d):
        return (z + d) % ZS

    def xpeer(d):
        return (x + d) % XS

    loads = [
        pltpu.make_async_copy(a, b, load_sem.at[i])
        for i, (a, b) in enumerate(((k_hbm, k), (v_hbm, v), (q_hbm, q)))
    ]
    for copy in loads:
        copy.start()

    barrier = pltpu.get_barrier_semaphore()
    mesh_id = pl.DeviceIdType.MESH
    pl.semaphore_signal(barrier, inc=1, device_id={"seq": partner}, device_id_type=mesh_id)
    for d in range(1, ZS):
        pl.semaphore_signal(
            barrier, inc=1, device_id={"seq": at(x, zpeer(d), c)}, device_id_type=mesh_id
        )
    for d in range(1, XS):
        pl.semaphore_signal(
            barrier, inc=1, device_id={"seq": at(xpeer(d), z, c)}, device_id_type=mesh_id
        )
    for d in range(1, YS):
        pl.semaphore_signal(
            barrier, inc=1, device_id={"tp": (y + d) % YS}, device_id_type=mesh_id
        )

    seedf[...] = seeds_ref[...].astype(F32)

    def make_table(h, _):
        row = seedf[pl.ds(h, 1), :]
        parts = []
        for g in range(feats // width):
            part = jnp.broadcast_to(row[:, g * width : (g + 1) * width], (width, width))
            parts.append(pltpu.roll(part, 0, 1, stride=1, stride_axis=0))
        table[h] = jnp.concatenate(parts, axis=1).astype(BF16)
        return 0

    lax.fori_loop(0, heads_here, make_table, 0)
    loads[0].wait()
    loads[1].wait()

    def state_head(phase, i, _):
        h = phase * per + i
        cols = pl.ds(pl.multiple_of(h * width, width), width)
        f = features(k[:, cols], table[h], scale)
        fk[h] = f
        st = lax.dot_general(
            v[:, cols], f, (((0,), (0,)), ((), ())), preferred_element_type=F32
        )
        for half in range(2):
            for part in range(2):
                start = (half * 2 + part) * rows
                own[phase, half, 2 * i + part] = st[start : start + rows]
        tot[pl.ds(h, 1), :] = jnp.sum(f.astype(F32), axis=0, keepdims=True)
        return 0

    pair = [
        remote(own.at[p, o], got.at[p], pair_s.at[p], pair_r.at[p], seq=partner) for p in range(2)
    ]
    tot_pair = remote(tot, tot_got, tp_s, tp_r, seq=partner)
    ups = [
        [
            remote(
                chip.at[p, zpeer(d)],
                up.at[p, z],
                up_s.at[p, d],
                up_r.at[p, d],
                seq=at(x, zpeer(d), c),
            )
            for d in range(1, ZS)
        ]
        for p in range(2)
    ]
    tot_ups = [
        remote(tot_chip, tot_up.at[z], tu_s.at[d], tu_r.at[d], seq=at(x, zpeer(d), c))
        for d in range(1, ZS)
    ]
    xs = [
        [
            remote(
                across.at[p, XS], across.at[p, x], x_s.at[p, d], x_r.at[p, d], seq=at(xpeer(d), z, c)
            )
            for d in range(1, XS)
        ]
        for p in range(2)
    ]
    tot_xs = [
        remote(tot_row, tot_across.at[x], tx_s.at[d], tx_r.at[d], seq=at(xpeer(d), z, c))
        for d in range(1, XS)
    ]
    downs = [
        [
            remote(
                down.at[p, zpeer(d)],
                back.at[p, z],
                down_s.at[p, d],
                down_r.at[p, d],
                seq=at(x, zpeer(d), c),
            )
            for d in range(1, ZS)
        ]
        for p in range(2)
    ]
    tot_fwd = remote(tot_half.at[0], tot_half.at[2], th_s, th_r, seq=partner)
    norms = [
        remote(norm, norm_got.at[y], n_s.at[d], n_r.at[d], tp=(y + d) % YS) for d in range(1, YS)
    ]

    lax.fori_loop(0, per, functools.partial(state_head, 0), 0)
    pl.semaphore_wait(barrier, 1 + (ZS - 1) + (XS - 1) + (YS - 1))
    pair[0].start()
    lax.fori_loop(0, per, functools.partial(state_head, 1), 0)
    pair[1].start()
    tot_pair.start()

    def send_up(p):
        pair[p].wait_recv()
        chip[p] = own[p, c] + got[p]
        for copy in ups[p]:
            copy.start()
        up[p, z] = chip[p, z]

    send_up(0)
    send_up(1)

    tot_pair.wait_recv()
    lanes = feats // 2

    def my_lanes(a):
        return jnp.where(c == 0, a[:, :lanes], a[:, lanes:])

    tot_chip[...] = my_lanes(tot[...] + tot_got[...])
    for copy in tot_ups:
        copy.start()
    tot_up[z] = tot_chip[...]

    loads[2].wait()
    causal = lax.broadcasted_iota(jnp.int32, (tok, tok), 0) >= lax.broadcasted_iota(
        jnp.int32, (tok, tok), 1
    )
    ones = jnp.ones((tok, width), BF16)

    def local_head(h, _):
        cols = pl.ds(pl.multiple_of(h * width, width), width)
        f = features(q[:, cols], table[h], scale)
        fq[h] = f
        scores = lax.dot_general(
            f, fk[h], (((1,), (1,)), ((), ())), preferred_element_type=F32
        )
        weights = jnp.where(causal, scores, 0.0).astype(BF16)
        numden[h] = jnp.dot(
            weights, jnp.concatenate([v[:, cols], ones], axis=1), preferred_element_type=F32
        )
        return 0

    def send_across(p):
        for copy in ups[p]:
            copy.wait_recv()
        total = up[p, 0]
        for i in range(1, ZS):
            total = total + up[p, i]
        across[p, XS] = total
        for copy in xs[p]:
            copy.start()
        across[p, x] = jnp.zeros_like(total)

    def send_down(p):
        for copy in xs[p]:
            copy.wait_recv()
        run = jnp.zeros((rows, feats), F32)
        for i in range(XS):
            run = run + jnp.where(i < x, across[p, i], 0.0)
        for i in range(ZS):
            down[p, i] = run
            if i < ZS - 1:
                run = run + up[p, i]
        for copy in downs[p]:
            copy.start()
        back[p, z] = down[p, z]

    lax.fori_loop(0, per, local_head, 0)
    send_across(0)
    lax.fori_loop(per, heads_here, local_head, 0)

    for copy in tot_ups:
        copy.wait_recv()
    run = jnp.zeros((heads_here, lanes), F32)
    before = run
    for i in range(ZS):
        before = before + jnp.where(i < z, tot_up[i], 0.0)
        run = run + tot_up[i]
    tot_row[...] = run
    for copy in tot_xs:
        copy.start()
    tot_across[x] = jnp.zeros_like(run)

    send_down(0)
    send_across(1)

    for copy in tot_xs:
        copy.wait_recv()
    for i in range(XS):
        before = before + jnp.where(i < x, tot_across[i], 0.0)
    tot_half[1] = before + jnp.where(c == 1, my_lanes(tot_got[...]), 0.0)
    tot_half[0] = before + jnp.where(c == 0, my_lanes(tot[...]), 0.0)
    tot_fwd.start()

    send_down(1)

    def piece(p, j):
        return remote(
            pass_on.at[p, j], full.at[p, c, j], fwd_s.at[p, j], fwd_r.at[p, j], seq=partner
        )

    def send_on(p):
        def one(j):
            base = back[p, j]
            pass_on[p, j] = base + jnp.where(c == 0, own[p, 0, j], 0.0)
            piece(p, j).start()
            full[p, c, j] = base + jnp.where(c == 1, got[p, j], 0.0)

        one(z)
        for d in range(1, ZS):
            downs[p][d - 1].wait_recv()
            one((z - d + ZS) % ZS)

    def finish(p):
        for j in range(ZS):
            piece(p, j).wait_recv()
        first, second = tot_half[1], tot_half[2]
        totals = jnp.concatenate(
            [jnp.where(c == 0, first, second), jnp.where(c == 0, second, first)], axis=1
        )
        seedf[...] = totals

        def head(i, acc):
            h = p * per + i
            parts = [
                full[p, half, 2 * i + part].astype(BF16) for half in range(2) for part in range(2)
            ]
            row = seedf[pl.ds(h, 1), :]
            parts.append(jnp.broadcast_to(row, (width, feats)).astype(BF16))
            prior = jnp.concatenate(parts, axis=0)
            nd = numden[h] + lax.dot_general(
                fq[h], prior, (((1,), (1,)), ((), ())), preferred_element_type=F32
            )
            out = nd[:, :width] / nd[:, width:]
            heads[h] = out
            return acc + out * out

        return head

    send_on(0)
    acc = jnp.zeros((tok, width), F32)
    tot_fwd.wait_recv()
    acc = lax.fori_loop(0, per, finish(0), acc)
    send_on(1)
    acc = lax.fori_loop(0, per, finish(1), acc)

    sums = jnp.sum(acc.T, axis=0, keepdims=True)
    norm[...] = jnp.broadcast_to(sums, norm.shape)
    for copy in norms:
        copy.start()
    norm_got[y] = norm[...]
    for copy in norms:
        copy.wait_recv()
    overall = norm_got[0]
    for i in range(1, YS):
        overall = overall + norm_got[i]
    factor = lax.rsqrt(overall / (columns * YS) + 1e-06)
    factor = jnp.broadcast_to(factor[:1], (width, tok)).T

    def scale_head(h, _):
        cols = pl.ds(pl.multiple_of(h * width, width), width)
        out_ref[:, cols] = (heads[h] * factor * gain_ref[pl.ds(h, 1), :]).astype(BF16)
        return 0

    lax.fori_loop(0, heads_here, scale_head, 0)

    for p in range(2):
        pair[p].wait_send()
        for copy in ups[p] + xs[p] + downs[p]:
            copy.wait_send()
        for j in range(ZS):
            piece(p, j).wait_send()
    tot_pair.wait_send()
    tot_fwd.wait_send()
    for copy in tot_ups + tot_xs + norms:
        copy.wait_send()


def per_device(queries, keys, values, seeds, gain):
    tok, columns = queries.shape
    heads_here, feats = seeds.shape
    width = columns // heads_here
    per = heads_here // 2
    rows = per * width // (2 * ZS)
    dma = pltpu.SemaphoreType.DMA
    vm = pltpu.VMEM
    hbm = pl.BlockSpec(memory_space=pl.ANY)
    onchip = pl.BlockSpec(memory_space=pltpu.VMEM)
    return pl.pallas_call(
        kernel,
        out_shape=jax.ShapeDtypeStruct((tok, columns), BF16),
        in_specs=[hbm, hbm, hbm, onchip, onchip],
        out_specs=onchip,
        scratch_shapes=[
            vm((tok, columns), BF16),
            vm((tok, columns), BF16),
            vm((tok, columns), BF16),
            vm((heads_here, feats), F32),
            vm((heads_here, width, feats), BF16),
            vm((heads_here, tok, feats), BF16),
            vm((heads_here, tok, feats), BF16),
            vm((heads_here, tok, 2 * width), F32),
            vm((heads_here, tok, width), F32),
            vm((2, 2, ZS, rows, feats), F32),
            vm((2, ZS, rows, feats), F32),
            vm((2, ZS, rows, feats), F32),
            vm((2, ZS, rows, feats), F32),
            vm((2, XS + 1, rows, feats), F32),
            vm((2, ZS, rows, feats), F32),
            vm((2, ZS, rows, feats), F32),
            vm((2, ZS, rows, feats), F32),
            vm((2, 2, ZS, rows, feats), F32),
            vm((heads_here, feats), F32),
            vm((heads_here, feats), F32),
            vm((heads_here, feats // 2), F32),
            vm((ZS, heads_here, feats // 2), F32),
            vm((heads_here, feats // 2), F32),
            vm((XS, heads_here, feats // 2), F32),
            vm((3, heads_here, feats // 2), F32),
            vm((8, tok), F32),
            vm((YS, 8, tok), F32),
            dma((3,)),
            dma((2,)),
            dma((2,)),
            dma((2, ZS)),
            dma((2, ZS)),
            dma((2, XS)),
            dma((2, XS)),
            dma((2, ZS)),
            dma((2, ZS)),
            dma((2, ZS)),
            dma((2, ZS)),
            dma,
            dma,
            dma((ZS,)),
            dma((ZS,)),
            dma((XS,)),
            dma((XS,)),
            dma,
            dma,
            dma((YS,)),
            dma((YS,)),
        ],
        compiler_params=pltpu.CompilerParams(collective_id=0, has_side_effects=True),
        name="prefix_attention",
    )(queries, keys, values, seeds, gain.reshape(heads_here, width))


def solution(mesh):
    placed = (P("seq", "tp"), P("seq", "tp"), P("seq", "tp"), P("tp", None), P("tp"))
    return jax.shard_map(
        per_device, mesh=mesh, in_specs=placed, out_specs=P("seq", "tp"), check_vma=False
    )
```

```python
import functools

import jax
import jax.numpy as jnp
from jax import lax
from jax.experimental import pallas as pl
from jax.experimental.pallas import tpu as pltpu
from jax.sharding import PartitionSpec as P

XS, ZS, CORES, YS = 4, 8, 2, 4
PHASES = 4
FAR_FIRST = (4, 3, 5, 2, 6, 1, 7)
TOTALS = PHASES // 2 - 1
F32, BF16 = jnp.float32, jnp.bfloat16


def remote(src, dst, send, recv, **where):
    return pltpu.make_async_remote_copy(
        src_ref=src,
        dst_ref=dst,
        send_sem=send,
        recv_sem=recv,
        device_id=where,
        device_id_type=pl.DeviceIdType.MESH,
    )


def features(x, table, scale):
    u = jnp.dot(x, table, preferred_element_type=F32) * scale
    return (jnp.maximum(u, 0.0) + jnp.exp(jnp.minimum(u, 0.0))).astype(BF16)


def kernel(
    q_hbm,
    k_hbm,
    v_hbm,
    seeds_ref,
    heads,
    factor_ref,
    q,
    k,
    v,
    seedf,
    table,
    fk,
    fq,
    numden,
    own,
    got,
    chip,
    up,
    across,
    down,
    back,
    pass_on,
    full,
    tot,
    tot_got,
    tot_chip,
    tot_up,
    tot_across,
    tot_down,
    tot_back,
    tot_on,
    tot_full,
    norm,
    load_sem,
    pair_s,
    pair_r,
    up_s,
    up_r,
    x_s,
    x_r,
    down_s,
    down_r,
    fwd_s,
    fwd_r,
    tp_s,
    tp_r,
    tu_s,
    tu_r,
    tx_s,
    tx_r,
    td_s,
    td_r,
    th_s,
    th_r,
    n_s,
    n_r,
):
    tok, columns = q.shape
    heads_here, _, feats = fk.shape
    width = columns // heads_here
    per = heads_here // PHASES
    rows = own.shape[3]
    blocks = ZS // per
    lanes = feats // 2
    scale = width ** (-0.25)
    s = lax.axis_index("seq")
    y = lax.axis_index("tp")
    c = s % CORES
    z = (s // CORES) % ZS
    x = s // (CORES * ZS)
    o = 1 - c

    def at(x_, z_, c_):
        return (x_ * ZS + z_) * CORES + c_

    partner = at(x, z, o)

    def zpeer(d):
        return (z + d) % ZS

    def xpeer(d):
        return (x + d) % XS

    def chunk(p):
        return slice(p * per * width, (p + 1) * per * width)

    k_loads = [
        pltpu.make_async_copy(k_hbm.at[:, chunk(p)], k.at[:, chunk(p)], load_sem.at[0, p])
        for p in range(PHASES)
    ]
    v_loads = [
        pltpu.make_async_copy(v_hbm.at[:, chunk(p)], v.at[:, chunk(p)], load_sem.at[1, p])
        for p in range(PHASES)
    ]
    q_load = pltpu.make_async_copy(q_hbm, q, load_sem.at[2, 0])
    for p in range(PHASES):
        k_loads[p].start()
        v_loads[p].start()
    q_load.start()

    barrier = pltpu.get_barrier_semaphore()
    mesh_id = pl.DeviceIdType.MESH
    pl.semaphore_signal(barrier, inc=1, device_id={"seq": partner}, device_id_type=mesh_id)
    for d in FAR_FIRST:
        pl.semaphore_signal(
            barrier, inc=1, device_id={"seq": at(x, zpeer(d), c)}, device_id_type=mesh_id
        )
    for d in range(1, XS):
        pl.semaphore_signal(
            barrier, inc=1, device_id={"seq": at(xpeer(d), z, c)}, device_id_type=mesh_id
        )
    for d in range(1, YS):
        pl.semaphore_signal(
            barrier, inc=1, device_id={"tp": (y + d) % YS}, device_id_type=mesh_id
        )

    seedf[...] = seeds_ref[...].astype(F32)

    def make_table(h):
        row = seedf[pl.ds(h, 1), :]
        parts = []
        for g in range(feats // width):
            part = jnp.broadcast_to(row[:, g * width : (g + 1) * width], (width, width))
            parts.append(pltpu.roll(part, 0, 1, stride=1, stride_axis=0))
        return jnp.concatenate(parts, axis=1).astype(BF16)

    def state_head(phase, i, _):
        h = phase * per + i
        cols = pl.ds(pl.multiple_of(h * width, width), width)
        circulant = make_table(h)
        table[h] = circulant
        f = features(k[:, cols], circulant, scale)
        fk[h] = f
        st = lax.dot_general(
            v[:, cols], f, (((0,), (0,)), ((), ())), preferred_element_type=F32
        )
        for half in range(2):
            for b in range(blocks):
                start = (half * blocks + b) * rows
                own[phase, half, blocks * i + b] = st[start : start + rows]
        sums = jnp.sum(f.astype(F32), axis=0, keepdims=True)
        for half in range(2):
            tot[half, h] = sums[:, half * lanes : (half + 1) * lanes]
        return 0

    everyone = range(PHASES)
    pair = [
        remote(own.at[p, o], got.at[p], pair_s.at[p], pair_r.at[p], seq=partner) for p in everyone
    ]
    tot_pair = remote(tot, tot_got, tp_s, tp_r, seq=partner)

    def over_z(src, dst, slot, send, recv):
        copies = [
            remote(src.at[zpeer(d)], dst.at[slot], send, recv, seq=at(x, zpeer(d), c))
            for d in FAR_FIRST
        ]
        all_but_one = pl.ds(0, ZS - 1)
        whole = remote(src.at[all_but_one], dst.at[all_but_one], send, recv, seq=partner)
        return copies, whole

    def over_x(slots, send, recv):
        copies = [
            remote(slots.at[XS], slots.at[x], send, recv, seq=at(xpeer(d), z, c)) for d in (2, 1, 3)
        ]
        all_but_one = pl.ds(0, XS - 1)
        whole = remote(slots.at[all_but_one], slots.at[all_but_one], send, recv, seq=partner)
        return copies, whole

    ups = [over_z(chip.at[p], up.at[p], z, up_s.at[p], up_r.at[p]) for p in everyone]
    xs = [over_x(across.at[p], x_s.at[p], x_r.at[p]) for p in everyone]
    downs = [over_z(down.at[p], back.at[p], z, down_s.at[p], down_r.at[p]) for p in everyone]
    forwards = [
        remote(pass_on.at[p], full.at[p, c], fwd_s.at[p], fwd_r.at[p], seq=partner)
        for p in everyone
    ]
    tot_ups = over_z(tot_chip, tot_up, z, tu_s, tu_r)
    tot_xs = over_x(tot_across, tx_s, tx_r)
    tot_downs = over_z(tot_down, tot_back, z, td_s, td_r)
    tot_fwd = remote(tot_on, tot_full.at[c], th_s, th_r, seq=partner)
    norms = [
        remote(norm.at[YS], norm.at[y], n_s, n_r, tp=(y + d) % YS) for d in (2, 1, 3)
    ]
    norm_whole = remote(
        norm.at[pl.ds(0, YS - 1)], norm.at[pl.ds(0, YS - 1)], n_s, n_r, seq=partner
    )

    def start(copies):
        for copy in copies[0]:
            copy.start()

    def arrive(copies):
        copies[1].wait_recv()

    def sent(copies):
        copies[1].wait_send()

    def states(p):
        k_loads[p].wait()
        v_loads[p].wait()
        lax.fori_loop(0, per, functools.partial(state_head, p), 0)
        if p == 0:
            pl.semaphore_wait(barrier, 1 + (ZS - 1) + (XS - 1) + (YS - 1))
        pair[p].start()

    def send_up(p):
        pair[p].wait_recv()
        chip[p] = own[p, c] + got[p]
        start(ups[p])
        up[p, z] = chip[p, z]

    def gather_row(copies, arrived, total, own_slot, cross):
        arrive(copies)
        t = arrived[0]
        for i in range(1, ZS):
            t = t + arrived[i]
        total[...] = t
        start(cross)
        own_slot[...] = jnp.zeros_like(t)

    def give_back(cross, slots, arrived, result, own_slot, copies):
        arrive(cross)
        base = jnp.where(0 < x, slots[0], 0.0)
        for i in range(1, XS):
            base = base + jnp.where(i < x, slots[i], 0.0)
        for i in range(ZS):
            result[i] = base
            if i < ZS - 1:
                base = base + arrived[i]
        start(copies)
        own_slot[...] = result[z]

    def send_across(p):
        gather_row(ups[p], up.at[p], across.at[p, XS], across.at[p, x], xs[p])

    def send_down(p):
        give_back(xs[p], across.at[p], up.at[p], down.at[p], back.at[p, z], downs[p])

    ones = jnp.ones((tok, width), BF16)

    def local_head(h, _):
        cols = pl.ds(pl.multiple_of(h * width, width), width)
        f = features(q[:, cols], table[h], scale)
        fq[h] = f
        scores = lax.dot_general(
            f, fk[h], (((1,), (1,)), ((), ())), preferred_element_type=F32
        )
        causal = lax.broadcasted_iota(jnp.int32, (tok, tok), 0) >= lax.broadcasted_iota(
            jnp.int32, (tok, tok), 1
        )
        weights = jnp.where(causal, scores, 0.0).astype(BF16)
        numden[h] = jnp.dot(
            weights, jnp.concatenate([v[:, cols], ones], axis=1), preferred_element_type=F32
        )
        return 0

    def local_heads(first, last):
        lax.fori_loop(first, last, local_head, 0)

    def send_on(p):
        arrive(downs[p])
        base = back[p]
        pass_on[p] = base + jnp.where(c == 0, own[p, 0], 0.0)
        forwards[p].start()
        full[p, c] = base + jnp.where(c == 1, got[p], 0.0)

    def finish(p, acc):
        forwards[p].wait_recv()

        def head(i, acc):
            h = p * per + i
            parts = [
                full[p, half, blocks * i + b].astype(BF16)
                for half in range(2)
                for b in range(blocks)
            ]
            row = jnp.concatenate([tot_full[0, h], tot_full[1, h]], axis=1)
            parts.append(jnp.broadcast_to(row, (width, feats)).astype(BF16))
            prior = jnp.concatenate(parts, axis=0)
            nd = numden[h] + lax.dot_general(
                fq[h], prior, (((1,), (1,)), ((), ())), preferred_element_type=F32
            )
            out = nd[:, :width] / nd[:, width:]
            heads[h] = out
            return acc + out * out

        return lax.fori_loop(0, per, head, acc)

    states(0)
    states(1)
    for p in range(2, PHASES):
        send_up(p - 2)
        states(p)
    tot_pair.start()
    send_up(PHASES - 2)
    tot_pair.wait_recv()
    tot_chip[...] = tot[c] + tot_got[c]
    start(tot_ups)
    tot_up[z] = tot_chip[z]
    send_up(PHASES - 1)

    q_load.wait()
    local_heads(0, heads_here - 2)
    for copy in pair + [tot_pair]:
        copy.wait_send()
    send_across(0)
    local_heads(heads_here - 2, heads_here)
    for p in range(1, PHASES):
        if p == PHASES - 1:
            gather_row(tot_ups, tot_up, tot_across.at[XS], tot_across.at[x], tot_xs)
        send_across(p)
        sent(ups[p - 1])
        if p == PHASES - 1:
            give_back(tot_xs, tot_across, tot_up, tot_down, tot_back.at[z], tot_downs)
        send_down(p - 1)
        sent(xs[p - 1])
    for copies in (ups[PHASES - 1], tot_ups, tot_xs):
        sent(copies)
    send_down(PHASES - 1)
    sent(xs[PHASES - 1])

    acc = jnp.zeros((tok, width), F32)
    for p in range(PHASES):
        send_on(p)
        if p == TOTALS:
            arrive(tot_downs)
            tot_on[...] = tot_back[...] + jnp.where(c == 0, tot[0], 0.0)
            tot_fwd.start()
            tot_full[c] = tot_back[...] + jnp.where(c == 1, tot_got[1], 0.0)
            sent(tot_downs)
        if p == TOTALS + 1:
            tot_fwd.wait_recv()
            for r in range(p):
                acc = finish(r, acc)
        if p > TOTALS + 1:
            acc = finish(p - 1, acc)
        sent(downs[p])
    for p in range(PHASES - 1):
        forwards[p].wait_send()
    tot_fwd.wait_send()
    acc = finish(PHASES - 1, acc)

    sums = jnp.sum(acc.T, axis=0, keepdims=True)
    norm[YS] = jnp.broadcast_to(sums, norm.shape[1:])
    for copy in norms:
        copy.start()
    norm[y] = norm[YS]
    norm_whole.wait_recv()
    overall = norm[0]
    for i in range(1, YS):
        overall = overall + norm[i]
    factor = lax.rsqrt(overall / (columns * YS) + 1e-06)
    factor = jnp.broadcast_to(factor[:1], (width, tok)).T

    factor_ref[...] = factor

    forwards[PHASES - 1].wait_send()
    norm_whole.wait_send()


def normalize(heads, factor, gain, out_hbm, out, sems):
    heads_here, _, width = heads.shape
    copies = []
    scale = factor[...]
    for h in range(heads_here):
        cols = slice(h * width, (h + 1) * width)
        out[:, cols] = (heads[h] * scale * gain[h : h + 1, :]).astype(BF16)
        copies.append(pltpu.make_async_copy(out.at[:, cols], out_hbm.at[:, cols], sems.at[h]))
        copies[-1].start()
    for copy in copies:
        copy.wait()


def per_device(queries, keys, values, seeds, gain):
    tok, columns = queries.shape
    heads_here, feats = seeds.shape
    width = columns // heads_here
    per = heads_here // PHASES
    rows = per * width // (2 * ZS)
    dma = pltpu.SemaphoreType.DMA
    vm = pltpu.VMEM
    hbm = pl.BlockSpec(memory_space=pl.ANY)
    onchip = pl.BlockSpec(memory_space=pltpu.VMEM)
    half = (heads_here, 1, feats // 2)
    heads, factor = pl.pallas_call(
        kernel,
        out_shape=(vm((heads_here, tok, width), F32), vm((tok, width), F32)),
        in_specs=[hbm, hbm, hbm, onchip],
        out_specs=(onchip, onchip),
        scratch_shapes=[
            vm((tok, columns), BF16),
            vm((tok, columns), BF16),
            vm((tok, columns), BF16),
            vm((heads_here, feats), F32),
            vm((heads_here, width, feats), BF16),
            vm((heads_here, tok, feats), BF16),
            vm((heads_here, tok, feats), BF16),
            vm((heads_here, tok, 2 * width), F32),
            vm((PHASES, 2, ZS, rows, feats), F32),
            vm((PHASES, ZS, rows, feats), F32),
            vm((PHASES, ZS, rows, feats), F32),
            vm((PHASES, ZS, rows, feats), F32),
            vm((PHASES, XS + 1, rows, feats), F32),
            vm((PHASES, ZS, rows, feats), F32),
            vm((PHASES, ZS, rows, feats), F32),
            vm((PHASES, ZS, rows, feats), F32),
            vm((PHASES, 2, ZS, rows, feats), F32),
            vm((2,) + half, F32),
            vm((2,) + half, F32),
            vm(half, F32),
            vm((ZS,) + half[1:], F32),
            vm((XS + 1,) + half[1:], F32),
            vm((ZS,) + half[1:], F32),
            vm((ZS,) + half[1:], F32),
            vm(half, F32),
            vm((2,) + half, F32),
            vm((YS + 1, 8, tok), F32),
            dma((3, PHASES)),
            dma((PHASES,)),
            dma((PHASES,)),
            dma((PHASES,)),
            dma((PHASES,)),
            dma((PHASES,)),
            dma((PHASES,)),
            dma((PHASES,)),
            dma((PHASES,)),
            dma((PHASES,)),
            dma((PHASES,)),
            dma,
            dma,
            dma,
            dma,
            dma,
            dma,
            dma,
            dma,
            dma,
            dma,
            dma,
            dma,
        ],
        compiler_params=pltpu.CompilerParams(collective_id=0, has_side_effects=True),
        name="prefix_attention",
    )(queries, keys, values, seeds)
    return pl.pallas_call(
        normalize,
        out_shape=jax.ShapeDtypeStruct((tok, columns), BF16),
        in_specs=[onchip, onchip, onchip],
        out_specs=hbm,
        scratch_shapes=[vm((tok, columns), BF16), dma((heads_here,))],
        name="normalize",
    )(
        pltpu.with_memory_space_constraint(heads, pltpu.VMEM),
        pltpu.with_memory_space_constraint(factor, pltpu.VMEM),
        gain.reshape(heads_here, width),
    )


def solution(mesh):
    placed = (P("seq", "tp"), P("seq", "tp"), P("seq", "tp"), P("tp", None), P("tp"))
    return jax.shard_map(
        per_device, mesh=mesh, in_specs=placed, out_specs=P("seq", "tp"), check_vma=False
    )
```

```python
import functools

import jax
import jax.numpy as jnp
from jax import lax
from jax.experimental import pallas as pl
from jax.experimental.pallas import tpu as pltpu
from jax.sharding import PartitionSpec as P

XS, ZS, CORES, YS = 4, 8, 2, 4
PHASES = 4
FAR_FIRST = (4, 3, 5, 2, 6, 1, 7)
TOTALS = PHASES // 2 - 1
F32, BF16 = jnp.float32, jnp.bfloat16


def remote(src, dst, send, recv, **where):
    return pltpu.make_async_remote_copy(
        src_ref=src,
        dst_ref=dst,
        send_sem=send,
        recv_sem=recv,
        device_id=where,
        device_id_type=pl.DeviceIdType.MESH,
    )


def features(x, table, scale):
    u = jnp.dot(x, table, preferred_element_type=F32) * scale
    return (jnp.maximum(u, 0.0) + jnp.exp(jnp.minimum(u, 0.0))).astype(BF16)


def kernel(
    q_hbm,
    k_hbm,
    v_hbm,
    seeds_ref,
    gain_ref,
    heads,
    factor_ref,
    q,
    k,
    v,
    seedf,
    table,
    fk,
    fq,
    numden,
    own,
    got,
    chip,
    up,
    across,
    down,
    back,
    pass_on,
    full,
    tot,
    tot_got,
    tot_chip,
    tot_up,
    tot_across,
    tot_down,
    tot_back,
    tot_on,
    tot_full,
    norm,
    load_sem,
    pair_s,
    pair_r,
    up_s,
    up_r,
    x_s,
    x_r,
    down_s,
    down_r,
    fwd_s,
    fwd_r,
    tp_s,
    tp_r,
    tu_s,
    tu_r,
    tx_s,
    tx_r,
    td_s,
    td_r,
    th_s,
    th_r,
    n_s,
    n_r,
):
    tok, columns = q.shape
    heads_here, _, feats = fk.shape
    width = columns // heads_here
    per = heads_here // PHASES
    rows = own.shape[3]
    blocks = ZS // per
    lanes = feats // 2
    scale = width ** (-0.25)
    s = lax.axis_index("seq")
    y = lax.axis_index("tp")
    c = lax.rem(s, CORES)
    z = lax.rem(lax.div(s, CORES), ZS)
    x = lax.div(s, CORES * ZS)
    o = 1 - c

    def at(x_, z_, c_):
        return (x_ * ZS + z_) * CORES + c_

    partner = at(x, z, o)

    def zpeer(d):
        return lax.rem(z + d, ZS)

    def xpeer(d):
        return lax.rem(x + d, XS)

    def chunk(p):
        return slice(p * per * width, (p + 1) * per * width)

    k_loads = [
        pltpu.make_async_copy(k_hbm.at[:, chunk(p)], k.at[:, chunk(p)], load_sem.at[0, p])
        for p in range(PHASES)
    ]
    v_loads = [
        pltpu.make_async_copy(v_hbm.at[:, chunk(p)], v.at[:, chunk(p)], load_sem.at[1, p])
        for p in range(PHASES)
    ]
    q_load = pltpu.make_async_copy(q_hbm, q, load_sem.at[2, 0])
    for p in range(PHASES):
        k_loads[p].start()
        v_loads[p].start()
    q_load.start()

    barrier = pltpu.get_barrier_semaphore()
    mesh_id = pl.DeviceIdType.MESH
    pl.semaphore_signal(barrier, inc=1, device_id={"seq": partner}, device_id_type=mesh_id)
    for d in FAR_FIRST:
        pl.semaphore_signal(
            barrier, inc=1, device_id={"seq": at(x, zpeer(d), c)}, device_id_type=mesh_id
        )
    for d in range(1, XS):
        pl.semaphore_signal(
            barrier, inc=1, device_id={"seq": at(xpeer(d), z, c)}, device_id_type=mesh_id
        )
    for d in range(1, YS):
        pl.semaphore_signal(
            barrier, inc=1, device_id={"tp": lax.rem(y + d, YS)}, device_id_type=mesh_id
        )

    seedf[...] = seeds_ref[...].astype(F32)

    def make_table(h):
        row = seedf[pl.ds(h, 1), :]
        parts = []
        for g in range(feats // width):
            part = jnp.broadcast_to(row[:, g * width : (g + 1) * width], (width, width))
            parts.append(pltpu.roll(part, 0, 1, stride=1, stride_axis=0))
        return jnp.concatenate(parts, axis=1).astype(BF16)

    def state_head(phase, i, _):
        h = phase * per + i
        cols = pl.ds(pl.multiple_of(h * width, width), width)
        circulant = make_table(h)
        table[h] = circulant
        f = features(k[:, cols], circulant, scale)
        fk[h] = f
        st = lax.dot_general(
            v[:, cols], f, (((0,), (0,)), ((), ())), preferred_element_type=F32
        )
        for half in range(2):
            for b in range(blocks):
                start = (half * blocks + b) * rows
                own[phase, half, blocks * i + b] = st[start : start + rows]
        sums = jnp.sum(f.astype(F32), axis=0, keepdims=True)
        for half in range(2):
            tot[half, h] = sums[:, half * lanes : (half + 1) * lanes]
        return 0

    everyone = range(PHASES)
    pair = [
        remote(own.at[p, o], got.at[p], pair_s.at[p], pair_r.at[p], seq=partner) for p in everyone
    ]
    tot_pair = remote(tot, tot_got, tp_s, tp_r, seq=partner)

    def over_z(src, dst, slot, send, recv):
        copies = [
            remote(src.at[zpeer(d)], dst.at[slot], send, recv, seq=at(x, zpeer(d), c))
            for d in FAR_FIRST
        ]
        all_but_one = pl.ds(0, ZS - 1)
        whole = remote(src.at[all_but_one], dst.at[all_but_one], send, recv, seq=partner)
        return copies, whole

    def over_x(slots, send, recv):
        copies = [
            remote(slots.at[XS], slots.at[x], send, recv, seq=at(xpeer(d), z, c)) for d in (2, 1, 3)
        ]
        all_but_one = pl.ds(0, XS - 1)
        whole = remote(slots.at[all_but_one], slots.at[all_but_one], send, recv, seq=partner)
        return copies, whole

    ups = [over_z(chip.at[p], up.at[p], z, up_s.at[p], up_r.at[p]) for p in everyone]
    xs = [over_x(across.at[p], x_s.at[p], x_r.at[p]) for p in everyone]
    downs = [over_z(down.at[p], back.at[p], z, down_s.at[p], down_r.at[p]) for p in everyone]
    forwards = [
        remote(pass_on.at[p], full.at[p, c], fwd_s.at[p], fwd_r.at[p], seq=partner)
        for p in everyone
    ]
    tot_ups = over_z(tot_chip, tot_up, z, tu_s, tu_r)
    tot_xs = over_x(tot_across, tx_s, tx_r)
    tot_downs = over_z(tot_down, tot_back, z, td_s, td_r)
    tot_fwd = remote(tot_on, tot_full.at[c], th_s, th_r, seq=partner)
    norms = [
        remote(norm.at[YS], norm.at[y], n_s, n_r, tp=lax.rem(y + d, YS)) for d in (2, 1, 3)
    ]
    norm_whole = remote(
        norm.at[pl.ds(0, YS - 1)], norm.at[pl.ds(0, YS - 1)], n_s, n_r, seq=partner
    )

    def start(copies):
        for copy in copies[0]:
            copy.start()

    def arrive(copies):
        copies[1].wait_recv()

    def sent(copies):
        copies[1].wait_send()

    def states(p):
        k_loads[p].wait()
        v_loads[p].wait()
        lax.fori_loop(0, per, functools.partial(state_head, p), 0, unroll=True)
        if p == 0:
            pl.semaphore_wait(barrier, 1 + (ZS - 1) + (XS - 1) + (YS - 1))
        pair[p].start()

    def send_up(p):
        pair[p].wait_recv()
        chip[p] = own[p, c] + got[p]
        start(ups[p])
        up[p, z] = chip[p, z]

    def gather_row(copies, arrived, total, own_slot, cross):
        arrive(copies)
        t = arrived[0]
        for i in range(1, ZS):
            t = t + arrived[i]
        total[...] = t
        start(cross)
        own_slot[...] = jnp.zeros_like(t)

    def give_back(cross, slots, arrived, result, own_slot, copies):
        arrive(cross)
        base = jnp.where(0 < x, slots[0], 0.0)
        for i in range(1, XS):
            base = base + jnp.where(i < x, slots[i], 0.0)
        for i in range(ZS):
            result[i] = base
            if i < ZS - 1:
                base = base + arrived[i]
        start(copies)
        own_slot[...] = result[z]

    def send_across(p):
        gather_row(ups[p], up.at[p], across.at[p, XS], across.at[p, x], xs[p])

    def send_down(p):
        give_back(xs[p], across.at[p], up.at[p], down.at[p], back.at[p, z], downs[p])

    ones = jnp.ones((tok, width), BF16)

    def local_head(h, _):
        cols = pl.ds(pl.multiple_of(h * width, width), width)
        f = features(q[:, cols], table[h], scale)
        fq[h] = f
        scores = lax.dot_general(
            f, fk[h], (((1,), (1,)), ((), ())), preferred_element_type=F32
        )
        causal = lax.broadcasted_iota(jnp.int32, (tok, tok), 0) >= lax.broadcasted_iota(
            jnp.int32, (tok, tok), 1
        )
        weights = jnp.where(causal, scores, 0.0).astype(BF16)
        numden[h] = jnp.dot(
            weights, jnp.concatenate([v[:, cols], ones], axis=1), preferred_element_type=F32
        )
        return 0

    def local_heads(first, last):
        lax.fori_loop(first, last, local_head, 0)

    def send_on(p):
        arrive(downs[p])
        base = back[p]
        pass_on[p] = base + jnp.where(c == 0, own[p, 0], 0.0)
        forwards[p].start()
        full[p, c] = base + jnp.where(c == 1, got[p], 0.0)

    def finish(p, acc):
        forwards[p].wait_recv()

        def head(i, acc):
            h = p * per + i
            parts = [
                full[p, half, blocks * i + b].astype(BF16)
                for half in range(2)
                for b in range(blocks)
            ]
            row = jnp.concatenate([tot_full[0, h], tot_full[1, h]], axis=1)
            parts.append(jnp.broadcast_to(row, (width, feats)).astype(BF16))
            prior = jnp.concatenate(parts, axis=0)
            nd = numden[h] + lax.dot_general(
                fq[h], prior, (((1,), (1,)), ((), ())), preferred_element_type=F32
            )
            out = nd[:, :width] / nd[:, width:]
            heads[h] = out * gain_ref[pl.ds(h, 1), :]
            return acc + out * out

        return lax.fori_loop(0, per, head, acc)

    states(0)
    states(1)
    for p in range(2, PHASES):
        send_up(p - 2)
        states(p)
    tot_pair.start()
    tot_pair.wait_recv()
    tot_chip[...] = tot[c] + tot_got[c]
    start(tot_ups)
    tot_up[z] = tot_chip[z]
    send_up(PHASES - 2)
    send_up(PHASES - 1)

    q_load.wait()
    local_heads(0, heads_here - 2)
    for copy in pair + [tot_pair]:
        copy.wait_send()
    send_across(0)
    local_heads(heads_here - 2, heads_here)
    for p in range(1, PHASES - 1):
        send_across(p)
        sent(ups[p - 1])
        if p == 1:
            gather_row(tot_ups, tot_up, tot_across.at[XS], tot_across.at[x], tot_xs)
        send_down(p - 1)
        sent(xs[p - 1])
    give_back(tot_xs, tot_across, tot_up, tot_down, tot_back.at[z], tot_downs)
    send_down(PHASES - 2)
    send_across(PHASES - 1)
    for copies in (ups[PHASES - 2], xs[PHASES - 2], ups[PHASES - 1], tot_ups, tot_xs):
        sent(copies)
    send_down(PHASES - 1)
    sent(xs[PHASES - 1])

    acc = jnp.zeros((tok, width), F32)
    for p in range(PHASES):
        send_on(p)
        if p == TOTALS:
            arrive(tot_downs)
            tot_on[...] = tot_back[...] + jnp.where(c == 0, tot[0], 0.0)
            tot_fwd.start()
            tot_full[c] = tot_back[...] + jnp.where(c == 1, tot_got[1], 0.0)
            sent(tot_downs)
        if p == TOTALS + 1:
            tot_fwd.wait_recv()
            for r in range(p):
                acc = finish(r, acc)
        if p > TOTALS + 1:
            acc = finish(p - 1, acc)
        sent(downs[p])
    for p in range(PHASES - 1):
        forwards[p].wait_send()
    tot_fwd.wait_send()
    acc = finish(PHASES - 1, acc)

    sums = jnp.sum(acc.T, axis=0, keepdims=True)
    norm[YS] = jnp.broadcast_to(sums, norm.shape[1:])
    for copy in norms:
        copy.start()
    norm[y] = norm[YS]
    norm_whole.wait_recv()
    overall = norm[0]
    for i in range(1, YS):
        overall = overall + norm[i]
    factor = lax.rsqrt(overall / (columns * YS) + 1e-06)
    factor = jnp.broadcast_to(factor[:1], (width, tok)).T

    factor_ref[...] = factor

    forwards[PHASES - 1].wait_send()
    norm_whole.wait_send()


def normalize(heads, factor, out_hbm, out, sems):
    heads_here, tok, width = heads.shape
    parts = sems.shape[0]
    size = tok // parts
    copies = []
    for i in range(parts):
        rows = pl.ds(i * size, size)
        scale = factor[rows, :]
        for h in range(heads_here):
            out[rows, h * width : (h + 1) * width] = (heads[h, rows, :] * scale).astype(BF16)
        copies.append(pltpu.make_async_copy(out.at[rows], out_hbm.at[rows], sems.at[i]))
        copies[-1].start()
    for copy in copies:
        copy.wait()


def per_device(queries, keys, values, seeds, gain):
    tok, columns = queries.shape
    heads_here, feats = seeds.shape
    width = columns // heads_here
    per = heads_here // PHASES
    rows = per * width // (2 * ZS)
    dma = pltpu.SemaphoreType.DMA
    vm = pltpu.VMEM
    hbm = pl.BlockSpec(memory_space=pl.ANY)
    onchip = pl.BlockSpec(memory_space=pltpu.VMEM)
    half = (heads_here, 1, feats // 2)
    heads, factor = pl.pallas_call(
        kernel,
        out_shape=(vm((heads_here, tok, width), F32), vm((tok, width), F32)),
        in_specs=[hbm, hbm, hbm, onchip, onchip],
        out_specs=(onchip, onchip),
        scratch_shapes=[
            vm((tok, columns), BF16),
            vm((tok, columns), BF16),
            vm((tok, columns), BF16),
            vm((heads_here, feats), F32),
            vm((heads_here, width, feats), BF16),
            vm((heads_here, tok, feats), BF16),
            vm((heads_here, tok, feats), BF16),
            vm((heads_here, tok, 2 * width), F32),
            vm((PHASES, 2, ZS, rows, feats), F32),
            vm((PHASES, ZS, rows, feats), F32),
            vm((PHASES, ZS, rows, feats), F32),
            vm((PHASES, ZS, rows, feats), F32),
            vm((PHASES, XS + 1, rows, feats), F32),
            vm((PHASES, ZS, rows, feats), F32),
            vm((PHASES, ZS, rows, feats), F32),
            vm((PHASES, ZS, rows, feats), F32),
            vm((PHASES, 2, ZS, rows, feats), F32),
            vm((2,) + half, F32),
            vm((2,) + half, F32),
            vm(half, F32),
            vm((ZS,) + half[1:], F32),
            vm((XS + 1,) + half[1:], F32),
            vm((ZS,) + half[1:], F32),
            vm((ZS,) + half[1:], F32),
            vm(half, F32),
            vm((2,) + half, F32),
            vm((YS + 1, 8, tok), F32),
            dma((3, PHASES)),
            dma((PHASES,)),
            dma((PHASES,)),
            dma((PHASES,)),
            dma((PHASES,)),
            dma((PHASES,)),
            dma((PHASES,)),
            dma((PHASES,)),
            dma((PHASES,)),
            dma((PHASES,)),
            dma((PHASES,)),
            dma,
            dma,
            dma,
            dma,
            dma,
            dma,
            dma,
            dma,
            dma,
            dma,
            dma,
            dma,
        ],
        compiler_params=pltpu.CompilerParams(collective_id=0, has_side_effects=True),
        name="prefix_attention",
    )(queries, keys, values, seeds, gain.reshape(heads_here, width))
    return pl.pallas_call(
        normalize,
        out_shape=jax.ShapeDtypeStruct((tok, columns), BF16),
        in_specs=[onchip, onchip],
        out_specs=hbm,
        scratch_shapes=[vm((tok, columns), BF16), dma((4,))],
        name="normalize",
    )(
        pltpu.with_memory_space_constraint(heads, pltpu.VMEM),
        pltpu.with_memory_space_constraint(factor, pltpu.VMEM),
    )


def solution(mesh):
    placed = (P("seq", "tp"), P("seq", "tp"), P("seq", "tp"), P("tp", None), P("tp"))
    return jax.shard_map(
        per_device, mesh=mesh, in_specs=placed, out_specs=P("seq", "tp"), check_vma=False
    )
```
